32 devices in a mesh: dp: 8 (over z, y), seq: 4 (over x, core).
Axes of the slice: x: 2, y: 2, z: 4, core: 2. Of those that a mesh axis runs over, the one named last changes fastest.
Arguments:
- inputs: bfloat16 [16, 2048, 256], P('dp', 'seq'), may hold values from -6 to 6
- timesteps: int32 [16], P('dp'), may hold values from 0 to 4999, as said below
- lengths: int32 [16], P('dp'), may hold values from 512 to 2048, as said below
- qkv_weight: bfloat16 [256, 768], replicated, may hold values from -0.375 to 0.375
- query_bias: float32 [256], replicated, may hold values from -1.75 to 1.75
- value_bias: float32 [256], replicated, may hold values from -0.1875 to 0.1875
- out_weight: bfloat16 [256, 256], replicated, may hold values from -3 to 3
- out_bias: float32 [256], replicated, may hold values from -1.75 to 1.75
- attn_gain: float32 [256], replicated, may hold values from 0.5 to 1.5
- attn_shift: float32 [256], replicated, may hold values from -1.25 to 1.25
- up_weight: bfloat16 [256, 1024], replicated, may hold values from -0.375 to 0.375
- up_bias: float32 [1024], replicated, may hold values from -1.75 to 1.75
- down_weight: bfloat16 [1024, 256], replicated, may hold values from -0.1875 to 0.1875
- down_bias: float32 [256], replicated, may hold values from -1.75 to 1.75
- ffn_gain: float32 [256], replicated, may hold values from 0.5 to 1.5
- ffn_shift: float32 [256], replicated, may hold values from -1.25 to 1.25
- cotangent: bfloat16 [16, 2048, 256], P('dp', 'seq'), may hold values from -6 to 6
Outputs:
- output: bfloat16 [16, 2048, 256], P('dp', 'seq')
- input_grad: float32 [16, 2048, 256], P('dp', 'seq')
- qkv_grad: float32 [256, 768], replicated
- qbias_grad: float32 [256], replicated
- vbias_grad: float32 [256], replicated
- wout_grad: float32 [256, 256], replicated
- obias_grad: float32 [256], replicated
- again_grad: float32 [256], replicated
- ashift_grad: float32 [256], replicated
- wup_grad: float32 [256, 1024], replicated
- ubias_grad: float32 [1024], replicated
- wdown_grad: float32 [1024, 256], replicated
- dbias_grad: float32 [256], replicated
- fgain_grad: float32 [256], replicated
- fshift_grad: float32 [256], replicated
The draws below stay inside these ranges and needn't reach their ends.
Inputs may be any that keep to these rules, and one draw needn't show every extreme that they name: High timesteps are more common than low ones. `lengths`: positions below an item's length are real, the rest padding that no query attends to; some item has exactly 2048 and some exactly 512.
All inputs are finite; a program needn't handle non-finite values.
Results may differ from the reference program's by a relative error of at most 0.015.
The reference program's roundings to bfloat16 on the way count: a program that leaves them out, or rounds other values in their place, can miss the bound.
Values may be sent and summed in bfloat16 or wider, within the bound.
No kernel may reach another device: no remote copies, remote signals or barrier semaphores. Data moves between devices by JAX's collectives and lax.ppermute only.
A program may use at most 64 MiB of HBM per device.

```python
import math
from functools import partial
import jax
import jax.numpy as jnp
from jax import lax

D = 256
H = 4
DH = 64
FF = 1024
TSTEPS = 5000
LEN = 2048
ITEMS = 16


def draw_timesteps(key, part):
    first_key, second_key = jax.random.split(jax.random.fold_in(key, 11))
    first_draw = jax.random.randint(first_key, (ITEMS,), 0, TSTEPS)
    second_draw = jax.random.randint(second_key, (ITEMS,), 0, TSTEPS)
    return jnp.maximum(first_draw, second_draw).astype(jnp.int32)


def draw_lengths(key, part):
    first_key, second_key = jax.random.split(jax.random.fold_in(key, 7))
    drawn = jax.random.randint(first_key, (ITEMS,), LEN // 4, LEN + 1)
    shuffled = jax.random.permutation(second_key, ITEMS)
    drawn = drawn.at[shuffled[0]].set(LEN).at[shuffled[1]].set(LEN // 4)
    return drawn.astype(jnp.int32)


def shard_levels(own_key, extent, cuts, least, largest):
    factor_of = 1.0
    for dim, shards_of in cuts:
        steps = jax.random.uniform(jax.random.fold_in(jax.random.fold_in(own_key, 6), dim), (shards_of,), jnp.float32, least / len(cuts), largest / len(cuts))
        factor_of = factor_of * jnp.repeat(jnp.exp(steps), extent[dim] // shards_of).reshape((-1,) + (1,) * (len(extent) - 1 - dim))
    return factor_of


def noise(rng, shape, deviation, reach, shards=(), kind=jnp.bfloat16):
    array = deviation * jax.random.normal(rng, shape, jnp.float32)
    if shards:
        array = array * shard_levels(rng, shape, shards, -0.22, 0.18)
    return jnp.clip(array, -reach, reach).astype(kind)


def setup_inputs(seed: int = 0) -> dict:
    keys = jax.random.split(jax.random.key(seed), 18)
    inputs = noise(keys[0], (ITEMS, LEN, D), 1.0, 6.0, ((0, 8), (1, 4)))
    timesteps = draw_timesteps(jax.random.fold_in(keys[17], 71), 0)
    lengths = draw_lengths(jax.random.fold_in(keys[17], 71), 0)
    qkv_weight = noise(keys[3], (D, 3 * D), D ** -0.5, 0.375)
    query_bias = noise(keys[4], (D,), 0.3, 1.75, (), jnp.float32)
    value_bias = noise(keys[5], (D,), 0.03, 0.1875, (), jnp.float32)
    out_weight = noise(keys[6], (D, D), (D // 64) ** -0.5, 3.0)
    out_bias = noise(keys[7], (D,), 0.3, 1.75, (), jnp.float32)
    attn_gain = jnp.clip(1.0 + 0.1 * jax.random.normal(keys[8], (D,), jnp.float32), 0.5, 1.5)
    attn_shift = noise(keys[9], (D,), 0.2, 1.25, (), jnp.float32)
    up_weight = noise(keys[10], (D, FF), D ** -0.5, 0.375)
    up_bias = noise(keys[11], (FF,), 0.3, 1.75, (), jnp.float32)
    down_weight = noise(keys[12], (FF, D), FF ** -0.5, 0.1875)
    down_bias = noise(keys[13], (D,), 0.3, 1.75, (), jnp.float32)
    ffn_gain = jnp.clip(1.0 + 0.1 * jax.random.normal(keys[14], (D,), jnp.float32), 0.5, 1.5)
    ffn_shift = noise(keys[15], (D,), 0.2, 1.25, (), jnp.float32)
    cotangent = noise(keys[16], (ITEMS, LEN, D), 1.0, 6.0, ((0, 8), (1, 4)))
    return {"inputs": inputs, "timesteps": timesteps, "lengths": lengths, "qkv_weight": qkv_weight, "query_bias": query_bias, "value_bias": value_bias, "out_weight": out_weight, "out_bias": out_bias, "attn_gain": attn_gain, "attn_shift": attn_shift, "up_weight": up_weight, "up_bias": up_bias, "down_weight": down_weight, "down_bias": down_bias, "ffn_gain": ffn_gain, "ffn_shift": ffn_shift, "cotangent": cotangent}


@jax.custom_vjp
def low(v):
    return lax.optimization_barrier(v.astype(jnp.bfloat16)).astype(jnp.float32)

@jax.custom_vjp
def low_back(v):
    return v

def low_keep(v):
    return (low(v), None)

def low_pass(kept, grad):
    return (grad,)

def back_keep(v):
    return (v, None)

def back_low(kept, grad):
    return (low(grad),)
low.defvjp(low_keep, low_pass)
low_back.defvjp(back_keep, back_low)
eps = 1e-05
highest = lax.Precision.HIGHEST

def matmul_hi(left, right):
    return jnp.dot(left, right, precision=highest)

def layer_norm(values, gain, shift):
    row_mean = lax.optimization_barrier(jnp.mean(values, axis=-1, keepdims=True))
    centered = values - row_mean
    variance = lax.optimization_barrier(jnp.mean(centered * centered, axis=-1, keepdims=True))
    return centered * lax.rsqrt(variance + eps) * gain + shift

def time_feature(timestep, width):
    half_width = width // 2
    frequency = jnp.exp(-math.log(10000.0) * jnp.arange(half_width, dtype=jnp.float32) / half_width)
    angles = timestep.astype(jnp.float32) * frequency
    return jnp.concatenate([jnp.sin(angles), jnp.cos(angles)])

def head_attend(head_data, length):
    queries, key_rows, value_rows = head_data
    scores = low_back(matmul_hi(queries, key_rows.T) * DH ** (-0.5))
    valid_keys = jnp.arange(LEN) < length
    scores = jnp.where(valid_keys[None, :], scores, -1e+30)
    row_max = lax.optimization_barrier(jnp.max(scores, axis=-1, keepdims=True))
    exponent = jnp.exp(scores - row_max)
    attn_prob = exponent / lax.optimization_barrier(jnp.sum(exponent, axis=-1, keepdims=True))
    return matmul_hi(low(attn_prob), value_rows)

def split_heads(values):
    return values.reshape(LEN, H, DH).transpose(1, 0, 2)

def forward(params, item_rows, timestep, length):
    qkv_weight, query_bias, value_bias, out_weight, out_bias, attn_gain, attn_shift, up_weight, up_bias, down_weight, down_bias, ffn_gain, ffn_shift = params
    stream = item_rows + time_feature(timestep, D)[None, :]
    projected = matmul_hi(low(stream), qkv_weight)
    queries = low(low_back(projected[:, :D] + query_bias))
    key_rows = low(low_back(projected[:, D:2 * D]))
    value_rows = low(low_back(projected[:, 2 * D:] + value_bias))
    per_head = lax.map(jax.checkpoint(partial(head_attend, length=length)), (split_heads(queries), split_heads(key_rows), split_heads(value_rows)))
    attended = low(low_back(per_head.transpose(1, 0, 2).reshape(LEN, D)))
    branch = low_back(matmul_hi(attended, out_weight) + out_bias)
    normed = layer_norm(stream + branch, attn_gain, attn_shift)
    up_pre = low_back(matmul_hi(low(normed), up_weight) + up_bias)
    gelu_out = low(jax.nn.gelu(up_pre, approximate=False))
    ffn_out = low_back(matmul_hi(gelu_out, down_weight) + down_bias)
    return layer_norm(normed + ffn_out, ffn_gain, ffn_shift)

def reference(inputs, timesteps, lengths, qkv_weight, query_bias, value_bias, out_weight, out_bias, attn_gain, attn_shift, up_weight, up_bias, down_weight, down_bias, ffn_gain, ffn_shift, cotangent):
    params = tuple((tensor.astype(jnp.float32) for tensor in (qkv_weight, query_bias, value_bias, out_weight, out_bias, attn_gain, attn_shift, up_weight, up_bias, down_weight, down_bias, ffn_gain, ffn_shift)))

    def one_item(summed, item_data):
        item_rows, timestep, length, cot_rows = item_data

        def local_forward(weights_in, rows_in):
            return forward(weights_in, rows_in, timestep, length)
        result, pullback = jax.vjp(local_forward, params, item_rows.astype(jnp.float32))
        gradients, rows_grad = pullback(cot_rows.astype(jnp.float32))
        summed = jax.tree.map(lambda left, right: left + right, summed, gradients)
        return (summed, (result.astype(jnp.bfloat16), rows_grad))
    zero_grads = jax.tree.map(jnp.zeros_like, params)
    summed, (output, input_grad) = lax.scan(one_item, zero_grads, (inputs, timesteps, lengths, cotangent))
    return (output, input_grad, summed[0], summed[1], summed[2], summed[3], summed[4], summed[5], summed[6], summed[7], summed[8], summed[9], summed[10], summed[11], summed[12])
```

```python
import math

import jax
import jax.numpy as jnp
from jax import lax
from jax.experimental import pallas as pl
from jax.experimental.pallas import tpu as pltpu
from jax.sharding import PartitionSpec as P

D = 256
DH = 64
HW = 128
eps = 1e-05
f32 = jnp.float32
bf16 = jnp.bfloat16

QB = 256
RB = 256


def dot(a, b):
    return jnp.dot(a, b, preferred_element_type=f32)


def dot_t(a, b):
    return lax.dot_general(a, b, (((1,), (1,)), ((), ())), preferred_element_type=f32)


def t_dot(a, b):
    return lax.dot_general(a, b, (((0,), (0,)), ((), ())), preferred_element_type=f32)


def time_feature(timestep, width):
    half_width = width // 2
    frequency = jnp.exp(-math.log(10000.0) * jnp.arange(half_width, dtype=f32) / half_width)
    angles = timestep.astype(f32) * frequency
    return jnp.concatenate([jnp.sin(angles), jnp.cos(angles)])


def head_rows(rows, head):
    lane = lax.broadcasted_iota(jnp.int32, rows.shape, 1)
    chosen = (lane < DH) if head == 0 else (lane >= DH)
    return jnp.where(chosen, rows.astype(f32), 0.0)


def pick(first, second):
    lane = lax.broadcasted_iota(jnp.int32, first.shape, 1)
    return jnp.where(lane < DH, first, second)


def attend_kernel(meta, x0, x1, x2, x3, tv, wq, wk, wv, qb, vb,
                  o_ref, lse_ref, q_ref, k_ref, v_ref, xl_ref, mask_ref, vext):
    step = pl.program_id(0)
    part = x0.shape[0]

    @pl.when(step == 0)
    def _():
        for j, rows in enumerate((x0, x1, x2, x3)):
            here = pl.ds(j * part, part)
            low = (rows[...].astype(f32) + tv[...]).astype(bf16)
            xl_ref[here, :] = low
            q = (dot(low, wq[...]) + qb[...]).astype(bf16)
            q_ref[here, :] = (q.astype(f32) * (DH ** -0.5)).astype(bf16)
            k_ref[here, :] = dot(low, wk[...]).astype(bf16)
            v = (dot(low, wv[...]) + vb[...]).astype(bf16)
            v_ref[here, :] = v
            vext[here, :HW] = v
            vext[here, HW:] = jnp.ones((part, HW), bf16)
            place = meta[2 + j] + lax.broadcasted_iota(jnp.int32, (1, part), 1)
            mask_ref[:, here] = jnp.where(place < meta[1], 0.0, -1e30)

    q = q_ref[pl.ds(pl.multiple_of(step * QB, QB), QB), :]
    outs = []
    logs = []
    for head in range(2):
        qh = head_rows(q, head).astype(bf16)
        s = dot_t(qh, k_ref[...]) + mask_ref[...]
        m = jnp.max(s, axis=-1, keepdims=True)
        p = jnp.exp(s - m)
        oe = dot(p.astype(bf16), vext[...])
        total = oe[:, HW:]
        outs.append(oe[:, :HW] / total)
        logs.append(m + jnp.log(total))
    o_ref[...] = pick(outs[0], outs[1]).astype(bf16)
    lse_ref[...] = pick(logs[0], logs[1])


def norm_parts(a):
    mean = jnp.mean(a, axis=-1, keepdims=True)
    centered = a - mean
    r = lax.rsqrt(jnp.mean(centered * centered, axis=-1, keepdims=True) + eps)
    return centered * r, r


def norm_back(e, xhat, r):
    return r * (e - jnp.mean(e, axis=-1, keepdims=True)
                - xhat * jnp.mean(e * xhat, axis=-1, keepdims=True))


def col_sum(a):
    return jnp.sum(a, axis=0, keepdims=True)


def middle_kernel(meta, xo, xr, co, cr, tv, mine, theirs, wom, wot, ob, ag, ash,
                  wup, ub, wdn, db, fg, fsh,
                  out_ref, first_ref, agm_ref, agt_ref, gdn, gup, gout, gvec):
    step = pl.program_id(0)
    half = pl.num_programs(0) // 2
    core = meta[0]

    @pl.when(step == 0)
    def _():
        gdn[...] = jnp.zeros_like(gdn)
        gup[...] = jnp.zeros_like(gup)
        gout[...] = jnp.zeros_like(gout)
        gvec[...] = jnp.zeros_like(gvec)

    near = step < half
    x = jnp.where(near, xo[...].astype(f32), xr[...].astype(f32))
    c = jnp.where(near, co[...].astype(f32), cr[...].astype(f32))
    stream = x + tv[...]
    am = mine[...]
    at = theirs[...]
    first_sum = stream + dot(am, wom[...]) + dot(at, wot[...]) + ob[...]
    xhat1, r1 = norm_parts(first_sum)
    normed = xhat1 * ag[...] + ash[...]
    nl = normed.astype(bf16)
    u = dot(nl, wup[...]) + ub[...]
    cdf = 0.5 * (1.0 + lax.erf(u * (2.0 ** -0.5)))
    gl = (u * cdf).astype(bf16)
    second_sum = normed + dot(gl, wdn[...]) + db[...]
    xhat2, r2 = norm_parts(second_sum)
    out_ref[...] = (xhat2 * fg[...] + fsh[...]).astype(bf16)
    sum_grad = norm_back(c * fg[...], xhat2, r2)
    fgr = sum_grad.astype(bf16)
    gdn[...] += t_dot(gl, fgr)
    gg = dot_t(fgr, wdn[...])
    pdf = jnp.exp(-0.5 * u * u) * ((2.0 * math.pi) ** -0.5)
    ug = (gg * (cdf + u * pdf)).astype(bf16)
    gup[...] += t_dot(nl, ug)
    normed_grad = sum_grad + dot_t(ug, wup[...])
    first_grad = norm_back(normed_grad * ag[...], xhat1, r1)
    first_ref[...] = first_grad
    bg = first_grad.astype(bf16)
    rows_m = pl.ds(pl.multiple_of(core * HW, HW), HW)
    rows_t = pl.ds(pl.multiple_of((1 - core) * HW, HW), HW)
    gout[rows_m, :] += t_dot(am, bg)
    gout[rows_t, :] += t_dot(at, bg)
    agm_ref[...] = dot_t(bg, wom[...]).astype(bf16)
    agt_ref[...] = dot_t(bg, wot[...]).astype(bf16)
    ub_sum = col_sum(ug.astype(f32))
    gvec[0:1, :] += col_sum(bg.astype(f32))
    gvec[1:2, :] += col_sum(normed_grad * xhat1)
    gvec[2:3, :] += col_sum(normed_grad)
    gvec[3:4, :] += col_sum(fgr.astype(f32))
    gvec[4:5, :] += col_sum(c * xhat2)
    gvec[5:6, :] += col_sum(c)
    for j in range(4):
        gvec[8 + j:9 + j, :] += ub_sum[:, j * D:(j + 1) * D]


def back_kernel(q, k, v, xl, mask, am, at, o, lse,
                dq_ref, dk_ref, dv_ref, gw_ref, gb_ref, dkt, dvt, dwq):
    step = pl.program_id(0)
    last = pl.num_programs(0) - 1
    half = pl.num_programs(0) // 2
    scaling = DH ** -0.5

    @pl.when(step == 0)
    def _():
        dkt[...] = jnp.zeros_like(dkt)
        dvt[...] = jnp.zeros_like(dvt)
        dwq[...] = jnp.zeros_like(dwq)
        gb_ref[...] = jnp.zeros_like(gb_ref)

    rows = pl.ds(pl.multiple_of(step * QB, QB), QB)
    qs = q[rows, :]
    do = jnp.where(step < half, am[...].astype(f32), at[...].astype(f32))
    prod = do * o[...].astype(f32)
    qgs = []
    for head in range(2):
        qh = head_rows(qs, head)
        doh = head_rows(do, head)
        qhb = qh.astype(bf16)
        dohb = doh.astype(bf16)
        row_dot = jnp.sum(head_rows(prod, head), axis=-1, keepdims=True)
        s = dot_t(qhb, k[...]) + mask[...]
        p = jnp.exp(s - lse[:, head * DH:head * DH + 1])
        dp = dot_t(dohb, v[...])
        ds = (p * (dp - row_dot)).astype(bf16)
        qgs.append(dot(ds, k[...]))
        dkt[...] += dot(qh.T.astype(bf16), ds)
        dvt[...] += dot(doh.T.astype(bf16), p.astype(bf16))
    dq = (pick(qgs[0], qgs[1]) * scaling).astype(bf16)
    dq_ref[...] = dq
    dwq[...] += t_dot(xl[rows, :], dq)
    gb_ref[0:1, :] += col_sum(dq.astype(f32))

    @pl.when(step == last)
    def _():
        dk = dkt[...].T.astype(bf16)
        dv = dvt[...].T.astype(bf16)
        dk_ref[...] = dk
        dv_ref[...] = dv
        gw_ref[0] = dwq[...]
        gw_ref[1] = t_dot(xl[...], dk)
        gw_ref[2] = t_dot(xl[...], dv)
        gb_ref[1:2, :] = col_sum(dv.astype(f32))


def input_kernel(meta, first, mq, mk, mv, tq, tk, tv, wqm, wkm, wvm, wqt, wkt, wvt, out_ref):
    acc = first[...]
    acc += dot_t(mq[...], wqm[...])
    acc += dot_t(mk[...], wkm[...])
    acc += dot_t(mv[...], wvm[...])
    acc += dot_t(tq[...], wqt[...])
    acc += dot_t(tk[...], wkt[...])
    acc += dot_t(tv[...], wvt[...])
    out_ref[...] = acc


def whole(shape):
    return pl.BlockSpec(shape, lambda i, *_: (0,) * len(shape))


def device_bits(dp_size, with_core):
    bits = ([("seq", 1, 4)] if with_core else []) + [("seq", 2, 4)]
    b = 1
    while b < dp_size:
        bits.append(("dp", b, dp_size))
        b *= 2
    return bits


def flip(x, axis, b, size):
    return lax.ppermute(x, axis, [(i, i ^ b) for i in range(size)])


def all_sum(x, bits):
    kept = []
    for axis, b, size in bits:
        n = x.shape[0] // 2
        bit = (lax.axis_index(axis) // b) % 2
        keep = lax.dynamic_slice_in_dim(x, bit * n, n, 0)
        send = lax.dynamic_slice_in_dim(x, (1 - bit) * n, n, 0)
        got = flip(send, axis, b, size)
        x = (keep.astype(f32) + got.astype(f32)).astype(x.dtype)
        kept.append((axis, b, size, bit))
    for axis, b, size, bit in kept[::-1]:
        got = flip(x, axis, b, size)
        x = jnp.concatenate([jnp.where(bit == 0, x, got), jnp.where(bit == 0, got, x)], 0)
    return x


def small_sum(x, bits):
    for axis, b, size in bits:
        x = x + flip(x, axis, b, size)
    return x


def body(inputs, timesteps, lengths, qkv_weight, query_bias, value_bias, out_weight, out_bias,
         attn_gain, attn_shift, up_weight, up_bias, down_weight, down_bias, ffn_gain, ffn_shift,
         cotangent):
    assert lax.axis_size("seq") == 4 and inputs.shape[0] == 2
    part = inputs.shape[1]
    length_all = 4 * part
    rows_here = 2 * part
    ff = up_weight.shape[1]
    dp_size = lax.axis_size("dp")
    seq = lax.axis_index("seq")
    chip = seq // 2
    core = seq % 2
    across = [(i, i ^ 2) for i in range(4)]
    beside = [(i, i ^ 1) for i in range(4)]

    def item(values, which):
        return lax.dynamic_index_in_dim(values, which, 0, keepdims=False)

    x_own = item(inputs, chip)
    x_far = lax.ppermute(item(inputs, 1 - chip), "seq", across)
    y_own = lax.ppermute(x_own, "seq", beside)
    y_far = lax.ppermute(x_far, "seq", beside)
    c_own = item(cotangent, chip)
    c_far = lax.ppermute(item(cotangent, 1 - chip), "seq", across)
    tv = time_feature(item(timesteps, chip), D)[None, :]
    length = item(lengths, chip)
    meta = jnp.stack([core, length] + [part * (seq ^ b) for b in (0, 2, 1, 3)]).astype(jnp.int32)
    row = lambda a: a.reshape(1, -1)

    steps = length_all // QB
    wcol = lambda j: pl.BlockSpec((D, HW), lambda i, m: (0, 2 * j + m[0]))
    full = (length_all, HW)
    attended, lse, q, k, v, xl, mask = pl.pallas_call(
        attend_kernel,
        grid_spec=pltpu.PrefetchScalarGridSpec(
            num_scalar_prefetch=1,
            grid=(steps,),
            in_specs=[whole((part, D))] * 4 + [whole((1, D))] + [wcol(0), wcol(1), wcol(2)]
            + [pl.BlockSpec((1, HW), lambda i, m: (0, m[0]))] * 2,
            out_specs=[pl.BlockSpec((QB, HW), lambda i, m: (i, 0))] * 2
            + [whole(full)] * 3 + [whole((length_all, D)), whole((1, length_all))],
            scratch_shapes=[pltpu.VMEM((length_all, 2 * HW), bf16)],
        ),
        out_shape=[
            jax.ShapeDtypeStruct(full, bf16),
            jax.ShapeDtypeStruct(full, f32),
            jax.ShapeDtypeStruct(full, bf16),
            jax.ShapeDtypeStruct(full, bf16),
            jax.ShapeDtypeStruct(full, bf16),
            jax.ShapeDtypeStruct((length_all, D), bf16),
            jax.ShapeDtypeStruct((1, length_all), f32),
        ],
        name="attend",
    )(meta, x_own, x_far, y_own, y_far, tv, qkv_weight, qkv_weight, qkv_weight,
      row(query_bias), row(value_bias))

    theirs = lax.ppermute(attended[rows_here:], "seq", beside)

    tiles = rows_here // RB
    half = tiles // 2
    near = pl.BlockSpec((RB, D), lambda i, m: (jnp.minimum(i, half - 1), 0))
    far = pl.BlockSpec((RB, D), lambda i, m: (jnp.maximum(i - half, 0), 0))
    tile = pl.BlockSpec((RB, D), lambda i, m: (i, 0))
    thin = pl.BlockSpec((RB, HW), lambda i, m: (i, 0))
    w_mine = pl.BlockSpec((HW, D), lambda i, m: (m[0], 0))
    w_theirs = pl.BlockSpec((HW, D), lambda i, m: (1 - m[0], 0))
    vec = whole((1, D))
    output, first_grad, ag_mine, ag_theirs, gdn, gup, gout, gvec = pl.pallas_call(
        middle_kernel,
        grid_spec=pltpu.PrefetchScalarGridSpec(
            num_scalar_prefetch=1,
            grid=(tiles,),
            in_specs=[near, far, near, far, vec, thin, thin, w_mine, w_theirs, vec, vec, vec,
                      whole((D, ff)), whole((1, ff)), whole((ff, D)), vec, vec, vec],
            out_specs=[tile, tile, thin, thin, whole((ff, D)), whole((D, ff)), whole((D, D)),
                       whole((16, D))],
        ),
        out_shape=[
            jax.ShapeDtypeStruct((rows_here, D), bf16),
            jax.ShapeDtypeStruct((rows_here, D), f32),
            jax.ShapeDtypeStruct((rows_here, HW), bf16),
            jax.ShapeDtypeStruct((rows_here, HW), bf16),
            jax.ShapeDtypeStruct((ff, D), f32),
            jax.ShapeDtypeStruct((D, ff), f32),
            jax.ShapeDtypeStruct((D, D), f32),
            jax.ShapeDtypeStruct((16, D), f32),
        ],
        name="middle",
    )(meta, x_own, x_far, c_own, c_far, tv, attended, theirs, out_weight, out_weight,
      row(out_bias), row(attn_gain), row(attn_shift), up_weight, row(up_bias), down_weight,
      row(down_bias), row(ffn_gain), row(ffn_shift))

    ag_other = lax.ppermute(ag_theirs, "seq", beside)
    out_far = lax.ppermute(output[part:], "seq", across)

    bhalf = steps // 2
    bnear = pl.BlockSpec((QB, HW), lambda i: (jnp.minimum(i, bhalf - 1), 0))
    bfar = pl.BlockSpec((QB, HW), lambda i: (jnp.maximum(i - bhalf, 0), 0))
    bthin = pl.BlockSpec((QB, HW), lambda i: (i, 0))
    dq, dk, dv, gw, gb = pl.pallas_call(
        back_kernel,
        grid=(steps,),
        in_specs=[whole(full)] * 3 + [whole((length_all, D)), whole((1, length_all)), bnear, bfar,
                                      bthin, bthin],
        out_specs=[bthin, whole(full), whole(full), whole((3, D, HW)), whole((8, HW))],
        out_shape=[
            jax.ShapeDtypeStruct(full, bf16),
            jax.ShapeDtypeStruct(full, bf16),
            jax.ShapeDtypeStruct(full, bf16),
            jax.ShapeDtypeStruct((3, D, HW), f32),
            jax.ShapeDtypeStruct((8, HW), f32),
        ],
        scratch_shapes=[pltpu.VMEM((HW, length_all), f32), pltpu.VMEM((HW, length_all), f32),
                        pltpu.VMEM((D, HW), f32)],
        name="back",
    )(q, k, v, xl, mask, ag_mine, ag_other, attended, lse)

    got = [lax.ppermute(a[rows_here:], "seq", beside) for a in (dq, dk, dv)]
    mcol = lambda j: pl.BlockSpec((D, HW), lambda i, m: (0, 2 * j + m[0]))
    tcol = lambda j: pl.BlockSpec((D, HW), lambda i, m: (0, 2 * j + 1 - m[0]))
    input_rows = pl.pallas_call(
        input_kernel,
        grid_spec=pltpu.PrefetchScalarGridSpec(
            num_scalar_prefetch=1,
            grid=(tiles,),
            in_specs=[tile] + [thin] * 6 + [mcol(0), mcol(1), mcol(2), tcol(0), tcol(1), tcol(2)],
            out_specs=tile,
        ),
        out_shape=jax.ShapeDtypeStruct((rows_here, D), f32),
        name="inputs",
    )(meta, first_grad, dq, dk, dv, *got, *([qkv_weight] * 6))
    grad_far = lax.ppermute(input_rows[part:].astype(bf16), "seq", across).astype(f32)

    def both(own, other):
        return jnp.stack([jnp.where(chip == 0, own, other), jnp.where(chip == 0, other, own)])

    result = both(output[:part], out_far)
    input_grad = both(input_rows[:part], grad_far)

    every = device_bits(dp_size, True)
    chips = device_bits(dp_size, False)
    big = all_sum(jnp.concatenate([gdn, gup.reshape(ff, D), gout], 0).astype(bf16), every)
    g_down = big[:ff].astype(f32)
    g_up = big[ff:2 * ff].reshape(D, ff).astype(f32)
    g_out = big[2 * ff:].astype(f32)
    gvec = small_sum(gvec, every)

    wide = all_sum(gw.reshape(3 * D, HW).astype(bf16), chips)
    wide_other = lax.ppermute(wide, "seq", beside)
    first = jnp.where(core == 0, wide, wide_other).reshape(3, D, 1, HW)
    second = jnp.where(core == 0, wide_other, wide).reshape(3, D, 1, HW)
    g_qkv = jnp.concatenate([first, second], 2).reshape(3, D, D)
    g_qkv = g_qkv.transpose(1, 0, 2).reshape(D, 3 * D).astype(f32)

    gb = small_sum(gb, chips)
    gb_other = lax.ppermute(gb, "seq", beside)
    gb = jnp.concatenate([jnp.where(core == 0, gb, gb_other), jnp.where(core == 0, gb_other, gb)], 1)
    return (
        result, input_grad, g_qkv, gb[0], gb[1], g_out, gvec[0], gvec[1], gvec[2],
        g_up, gvec[8:12].reshape(ff), g_down, gvec[3], gvec[4], gvec[5],
    )


def solution(mesh):
    rows = P("dp", "seq", None)
    in_specs = (rows, P("dp"), P("dp")) + (P(),) * 13 + (rows,)
    out_specs = (rows, rows) + (P(),) * 13
    return jax.shard_map(body, mesh=mesh, in_specs=in_specs, out_specs=out_specs, check_vma=False)
```

```python
import math

import jax
import jax.numpy as jnp
from jax import lax
from jax.experimental import pallas as pl
from jax.experimental.pallas import tpu as pltpu
from jax.sharding import PartitionSpec as P

D = 256
DH = 64
HW = 128
eps = 1e-05
f32 = jnp.float32
bf16 = jnp.bfloat16

QB = 256
RB = 256


def dot(a, b):
    return jnp.dot(a, b, preferred_element_type=f32)


def dot_t(a, b):
    return lax.dot_general(a, b, (((1,), (1,)), ((), ())), preferred_element_type=f32)


def t_dot(a, b):
    return lax.dot_general(a, b, (((0,), (0,)), ((), ())), preferred_element_type=f32)


def time_feature(timestep, width):
    half_width = width // 2
    frequency = jnp.exp(-math.log(10000.0) * jnp.arange(half_width, dtype=f32) / half_width)
    angles = timestep.astype(f32) * frequency
    return jnp.concatenate([jnp.sin(angles), jnp.cos(angles)])


def head_rows(rows, head):
    lane = lax.broadcasted_iota(jnp.int32, rows.shape, 1)
    chosen = (lane < DH) if head == 0 else (lane >= DH)
    return jnp.where(chosen, rows.astype(f32), 0.0)


def pick(first, second):
    lane = lax.broadcasted_iota(jnp.int32, first.shape, 1)
    return jnp.where(lane < DH, first, second)


def lanes(shape):
    return lax.broadcasted_iota(jnp.int32, shape, 1)


def wide_queries(q, head, extra):
    lane = lanes(q.shape)
    own = (lane < DH) if head == 0 else (lane >= DH)
    spare = DH * (1 - head)
    high = q.astype(bf16)
    low = (q - high.astype(f32)).astype(bf16)
    first = jnp.where(own, high.astype(f32), jnp.where(lane == spare, 1.0, 0.0))
    for j, column in enumerate(extra):
        first = jnp.where(lane == spare + 1 + j, column, first)
    second = jnp.where(own, low.astype(f32), 0.0)
    return jnp.concatenate([first, second], 1).astype(bf16)


def wide_keys(k, bias, head):
    lane = lanes(k.shape)
    own = (lane < DH) if head == 0 else (lane >= DH)
    spare = DH * (1 - head)
    ones = (lane > spare) & (lane < spare + 4)
    first = jnp.where(own, k, jnp.where(lane == spare, bias, jnp.where(ones, 1.0, 0.0)))
    second = jnp.where(own, k, 0.0)
    return jnp.concatenate([first, second], 1).astype(bf16)


LOG2E = 1.4426950408889634


def attend_rows(q, kx, vext, o_ref, lse_ref):
    outs = []
    logs = []
    q2 = q.astype(f32) * LOG2E
    for head in range(2):
        s = dot_t(wide_queries(q2, head, ()), kx[head])
        m = jnp.max(s, axis=-1, keepdims=True)
        p = jnp.exp2(s - m)
        oe = dot(p.astype(bf16), vext[...])
        total = oe[:, HW:]
        outs.append(oe[:, :HW] / total)
        logs.append(m + jnp.log2(total))
    o_ref[...] = pick(outs[0], outs[1]).astype(bf16)
    lse_ref[...] = pick(logs[0], logs[1])


def attend_first(meta, x0, x1, x2, x3, tv, wq, wk, wv, qb, vb,
                 o_ref, lse_ref, q_ref, k_ref, kx, vext, xl_ref):
    step = pl.program_id(0)
    part = x0.shape[0]

    @pl.when(step == 0)
    def _():
        for j, rows in enumerate((x0, x1, x2, x3)):
            here = pl.ds(j * part, part)
            low = (rows[...].astype(f32) + tv[...]).astype(bf16)
            xl_ref[here, :] = low
            q = (dot(low, wq[...]) + qb[...]).astype(bf16)
            q_ref[here, :] = (q.astype(f32) * (DH ** -0.5)).astype(bf16)
            k = dot(low, wk[...]).astype(bf16)
            k_ref[here, :] = k
            place = meta[3 + j] + lax.broadcasted_iota(jnp.int32, k.shape, 0)
            bias = jnp.where(place < meta[2], 0.0, -1e30)
            for head in range(2):
                kx[head, here, :] = wide_keys(k.astype(f32), bias, head)
            vext[here, :HW] = (dot(low, wv[...]) + vb[...]).astype(bf16)
            vext[here, HW:] = jnp.ones((part, HW), bf16)

    start = pl.multiple_of(2 * part + step * QB, QB)
    attend_rows(q_ref[pl.ds(start, QB), :], kx, vext, o_ref, lse_ref)


def attend_second(q_ref, kx, vext, o_ref, lse_ref):
    attend_rows(q_ref[...], kx, vext, o_ref, lse_ref)


def norm_parts(a):
    mean = jnp.mean(a, axis=-1, keepdims=True)
    centered = a - mean
    r = lax.rsqrt(jnp.mean(centered * centered, axis=-1, keepdims=True) + eps)
    return centered * r, r


def norm_back(e, xhat, r):
    return r * (e - jnp.mean(e, axis=-1, keepdims=True)
                - xhat * jnp.mean(e * xhat, axis=-1, keepdims=True))


def col_sum(a):
    return jnp.sum(a, axis=0, keepdims=True)


def middle_kernel(meta, xo, xr, co, cr, tv, mine, theirs, wom, wot, ob, ag, ash,
                  wup, ub, wdn, db, fg, fsh,
                  out_ref, first_ref, agm_ref, agt_ref, keep_ref, send_ref, gvec, gdn, gup, gout, pack):
    step = pl.program_id(0)
    half = pl.num_programs(0) // 2
    core = meta[0]

    @pl.when(step == 0)
    def _():
        gdn[...] = jnp.zeros_like(gdn)
        gup[...] = jnp.zeros_like(gup)
        gout[...] = jnp.zeros_like(gout)
        gvec[...] = jnp.zeros_like(gvec)

    near = step < half
    x = jnp.where(near, xo[...].astype(f32), xr[...].astype(f32))
    c = jnp.where(near, co[...].astype(f32), cr[...].astype(f32))
    stream = x + tv[...]
    am = mine[...]
    at = theirs[...]
    first_sum = stream + dot(am, wom[...]) + dot(at, wot[...]) + ob[...]
    xhat1, r1 = norm_parts(first_sum)
    normed = xhat1 * ag[...] + ash[...]
    nl = normed.astype(bf16)
    u = dot(nl, wup[...]) + ub[...]
    cdf = 0.5 * (1.0 + lax.erf(u * (2.0 ** -0.5)))
    gl = (u * cdf).astype(bf16)
    second_sum = normed + dot(gl, wdn[...]) + db[...]
    xhat2, r2 = norm_parts(second_sum)
    out_ref[...] = (xhat2 * fg[...] + fsh[...]).astype(bf16)
    sum_grad = norm_back(c * fg[...], xhat2, r2)
    fgr = sum_grad.astype(bf16)
    gdn[...] += t_dot(gl, fgr)
    gg = dot_t(fgr, wdn[...])
    pdf = jnp.exp(-0.5 * u * u) * ((2.0 * math.pi) ** -0.5)
    ug = (gg * (cdf + u * pdf)).astype(bf16)
    gup[...] += t_dot(nl, ug)
    normed_grad = sum_grad + dot_t(ug, wup[...])
    first_grad = norm_back(normed_grad * ag[...], xhat1, r1)
    first_ref[...] = first_grad
    bg = first_grad.astype(bf16)
    rows_m = pl.ds(pl.multiple_of(core * HW, HW), HW)
    rows_t = pl.ds(pl.multiple_of((1 - core) * HW, HW), HW)
    gout[rows_m, :] += t_dot(am, bg)
    gout[rows_t, :] += t_dot(at, bg)
    agm_ref[...] = dot_t(bg, wom[...]).astype(bf16)
    agt_ref[...] = dot_t(bg, wot[...]).astype(bf16)
    ub_sum = col_sum(ug.astype(f32))
    gvec[0:1, :] += col_sum(bg.astype(f32))
    gvec[1:2, :] += col_sum(normed_grad * xhat1)
    gvec[2:3, :] += col_sum(normed_grad)
    gvec[3:4, :] += col_sum(fgr.astype(f32))
    gvec[4:5, :] += col_sum(c * xhat2)
    gvec[5:6, :] += col_sum(c)
    for j in range(4):
        gvec[8 + j:9 + j, :] += ub_sum[:, j * D:(j + 1) * D]

    @pl.when(step == pl.num_programs(0) - 1)
    def _():
        at = 0
        for grad in (gdn, gup, gout):
            n = grad.shape[0]
            for j in range(grad.shape[1] // HW):
                pack[at:at + n, :] = grad[:, j * HW:(j + 1) * HW].astype(bf16)
                at += n
        n = at // 2
        keep_ref[...] = pack[pl.ds(pl.multiple_of(core * n, HW), n), :]
        send_ref[...] = pack[pl.ds(pl.multiple_of((1 - core) * n, HW), n), :]


def back_rows(qs, do, lse, k, kx, vext, xl, dq_ref, dkt, dvt, dwq, dbq):
    scaling = DH ** -0.5
    qgs = []
    qf = qs.astype(f32)
    dof = do.astype(f32)
    q_t = qf.T.astype(bf16)
    do_t = dof.T.astype(bf16)
    for head in range(2):
        own = slice(head * DH, (head + 1) * DH)
        shift = -lse[:, head * DH:head * DH + 1]
        extra = []
        for _ in range(3):
            extra.append(shift.astype(bf16).astype(f32))
            shift = shift - extra[-1]
        p = jnp.exp2(dot_t(wide_queries(qf * LOG2E, head, extra), kx[head]))
        dvt[own, :] += dot(do_t[own], p.astype(bf16))
        dp = dot_t(head_rows(do, head).astype(bf16), vext[:, :HW])
        t = p * dp
        ds = (t - p * jnp.sum(t, axis=-1, keepdims=True)).astype(bf16)
        qgs.append(dot(ds, k[...]))
        dkt[own, :] += dot(q_t[own], ds)
    dq = (pick(qgs[0], qgs[1]) * scaling).astype(bf16)
    dq_ref[...] = dq
    dwq[...] += t_dot(xl, dq)
    dbq[...] += col_sum(dq.astype(f32))


def back_first(q, k, kx, vext, xl, do, lse, dq_ref, dkt, dvt, dwq, dbq):
    @pl.when(pl.program_id(0) == 0)
    def _():
        dkt[...] = jnp.zeros_like(dkt)
        dvt[...] = jnp.zeros_like(dvt)
        dwq[...] = jnp.zeros_like(dwq)
        dbq[...] = jnp.zeros_like(dbq)

    back_rows(q[...], do[...], lse[...], k, kx, vext, xl[...], dq_ref, dkt, dvt, dwq, dbq)


def back_second(meta, q, k, kx, vext, xl, do, lse, dkt0, dvt0, dwq0, dbq0, gvec,
                dq_ref, dk_ref, dv_ref, keep_ref, send_ref, dkt, dvt, dwq, dbq, pack):
    step = pl.program_id(0)
    chip = meta[1]

    @pl.when(step == 0)
    def _():
        dkt[...] = dkt0[...]
        dvt[...] = dvt0[...]
        dwq[...] = dwq0[...]
        dbq[...] = dbq0[...]

    first = pl.multiple_of(q.shape[0] * (pl.num_programs(0) + step), QB)
    back_rows(q[...], do[...], lse[...], k, kx, vext, xl[pl.ds(first, QB), :],
              dq_ref, dkt, dvt, dwq, dbq)

    @pl.when(step == pl.num_programs(0) - 1)
    def _():
        dk = dkt[...].T.astype(bf16)
        dv = dvt[...].T.astype(bf16)
        dk_ref[...] = dk
        dv_ref[...] = dv
        pack[0:D, :] = dwq[...].astype(bf16)
        pack[D:2 * D, :] = t_dot(xl[...], dk).astype(bf16)
        pack[2 * D:3 * D, :] = t_dot(xl[...], dv).astype(bf16)
        pack[3 * D:, :] = jnp.zeros((D, HW), bf16)
        extra = jnp.concatenate([gvec[:, :HW], gvec[:, HW:], dbq[...],
                                 col_sum(dv.astype(f32)), jnp.zeros((14, HW), f32)], 0)
        pack[3 * D:3 * D + 48, :] = extra.astype(bf16)
        n = 2 * D
        keep_ref[...] = pack[pl.ds(pl.multiple_of(chip * n, HW), n), :]
        send_ref[...] = pack[pl.ds(pl.multiple_of((1 - chip) * n, HW), n), :]


def input_kernel(meta, first, mq, mk, mv, tq, tk, tv, wqm, wkm, wvm, wqt, wkt, wvt, out_ref):
    acc = first[...]
    mine = jnp.concatenate([mq[...], mk[...], mv[...]], 1)
    theirs = jnp.concatenate([tq[...], tk[...], tv[...]], 1)
    acc += dot_t(mine, jnp.concatenate([wqm[...], wkm[...], wvm[...]], 1))
    acc += dot_t(theirs, jnp.concatenate([wqt[...], wkt[...], wvt[...]], 1))
    out_ref[...] = acc.astype(out_ref.dtype)


def unpack_kernel(meta, a_own, a_far, b_own, b_far,
                  down, up, out, qkv, ub, *rest):
    vecs = rest[:8]
    pack, wide = rest[8:]
    core = meta[0]
    chip = meta[1]
    n = pack.shape[0] // 4
    m = wide.shape[1] // 2
    for got, c, x in ((a_own, core, chip), (a_far, core, 1 - chip),
                      (b_own, 1 - core, chip), (b_far, 1 - core, 1 - chip)):
        pack[pl.ds(pl.multiple_of((2 * c + x) * n, HW), n), :] = got[:n, :]
        wide[c, pl.ds(pl.multiple_of(x * m, HW), m), :] = got[n:, :]
    at = 0
    for grad in (down, up, out):
        k = grad.shape[0]
        for j in range(grad.shape[1] // HW):
            grad[:, j * HW:(j + 1) * HW] = pack[at:at + k, :].astype(f32)
            at += k
    for j in range(3):
        for c in range(2):
            place = (2 * j + c) * HW
            qkv[:, place:place + HW] = wide[c, j * D:(j + 1) * D, :].astype(f32)
    both = wide[0, 3 * D:3 * D + 32, :].astype(f32) + wide[1, 3 * D:3 * D + 32, :].astype(f32)
    for i in range(6):
        vecs[i][:, :HW] = both[i:i + 1]
        vecs[i][:, HW:] = both[16 + i:17 + i]
    for j in range(4):
        ub[:, 2 * j * HW:(2 * j + 1) * HW] = both[8 + j:9 + j]
        ub[:, (2 * j + 1) * HW:(2 * j + 2) * HW] = both[24 + j:25 + j]
    for c in range(2):
        ends = wide[c, 3 * D + 32:3 * D + 48, :].astype(f32)
        vecs[6][:, c * HW:(c + 1) * HW] = ends[0:1]
        vecs[7][:, c * HW:(c + 1) * HW] = ends[1:2]


def whole(shape):
    return pl.BlockSpec(shape, lambda i, *_: (0,) * len(shape))


def dp_bits(dp_size):
    bits = []
    b = 1
    while b < dp_size:
        bits.append(b)
        b *= 2
    return bits


def halves(x, bit):
    n = x.shape[0] // 2
    return (lax.dynamic_slice_in_dim(x, bit * n, n, 0),
            lax.dynamic_slice_in_dim(x, (1 - bit) * n, n, 0))


def add_low(a, b):
    return (a.astype(f32) + b.astype(f32)).astype(bf16)


def dp_groups(dp_size):
    bits = dp_bits(dp_size)
    return [bits[:1]] + [bits[i:i + 2] for i in range(1, len(bits), 2)]


def position(index, group):
    return sum(((index // b) % 2) * 2 ** j for j, b in enumerate(group))


def flips(group):
    return [sum(b for j, b in enumerate(group) if (c >> j) & 1) for c in range(2 ** len(group))]


def dp_flip(x, mask, dp_size):
    return lax.ppermute(x, "dp", [(i, i ^ mask) for i in range(dp_size)])


def scatter_group(x, group, dp_size):
    at = position(lax.axis_index("dp"), group)
    n = x.shape[0] // 2 ** len(group)
    acc = lax.dynamic_slice_in_dim(x, at * n, n, 0).astype(f32)
    for c, mask in list(enumerate(flips(group)))[1:]:
        send = lax.dynamic_slice_in_dim(x, (at ^ c) * n, n, 0)
        acc = acc + dp_flip(send, mask, dp_size).astype(f32)
    return acc.astype(bf16)


def gather_group(x, group, dp_size):
    at = position(lax.axis_index("dp"), group)
    pieces = [x] + [dp_flip(x, mask, dp_size) for mask in flips(group)[1:]]
    out = []
    for j in range(len(pieces)):
        piece = pieces[j]
        for c in range(1, len(pieces)):
            piece = jnp.where(at == c, pieces[j ^ c], piece)
        out.append(piece)
    return jnp.concatenate(out, 0)


def cost(flops, transcendentals=0):
    return pl.CostEstimate(flops=flops, bytes_accessed=4 << 20, transcendentals=transcendentals)


def body(inputs, timesteps, lengths, qkv_weight, query_bias, value_bias, out_weight, out_bias,
         attn_gain, attn_shift, up_weight, up_bias, down_weight, down_bias, ffn_gain, ffn_shift,
         cotangent):
    assert lax.axis_size("seq") == 4 and inputs.shape[0] == 2
    part = inputs.shape[1]
    length_all = 4 * part
    rows_here = 2 * part
    ff = up_weight.shape[1]
    dp_size = lax.axis_size("dp")
    seq = lax.axis_index("seq")
    chip = seq // 2
    core = seq % 2
    across = [(i, i ^ 2) for i in range(4)]
    beside = [(i, i ^ 1) for i in range(4)]

    def item(values, which):
        return lax.dynamic_index_in_dim(values, which, 0, keepdims=False)

    x_out = item(inputs, 1 - chip)
    x_far = lax.ppermute(x_out, "seq", across)
    inputs, cotangent, timesteps, lengths, _ = lax.optimization_barrier(
        (inputs, cotangent, timesteps, lengths, x_out))
    x_own = item(inputs, chip)
    y_own = lax.ppermute(x_own, "seq", beside)
    c_own = item(cotangent, chip)
    c_out = item(cotangent, 1 - chip)
    tv = time_feature(jnp.where(chip == 0, timesteps[0], timesteps[1]), D)[None, :]
    slot = jnp.arange(8, dtype=jnp.int32)
    order = jnp.where(slot == 4, 2, jnp.where(slot == 5, 1, jnp.where(slot == 6, 3, 0)))
    meta = part * (seq ^ order)
    length = jnp.where(chip == 0, lengths[0], lengths[1])
    meta = jnp.where(slot == 0, core, jnp.where(slot == 1, chip, jnp.where(slot == 2, length, meta)))
    meta = meta.astype(jnp.int32)
    x_far, x_own, tv, meta, c_own, c_out = lax.optimization_barrier(
        (x_far, x_own, tv, meta, c_own, c_out))
    y_far = lax.ppermute(x_far, "seq", beside)
    c_far = lax.ppermute(c_out, "seq", across)
    row = lambda a: a.reshape(1, -1)

    steps = rows_here // QB
    wcol = lambda j: pl.BlockSpec((D, HW), lambda i, m: (0, 2 * j + m[0]))
    thin = pl.BlockSpec((QB, HW), lambda i, *_: (i, 0))
    later = pl.BlockSpec((QB, HW), lambda i, *_: (i + steps, 0))
    full = (length_all, HW)
    pair = [jax.ShapeDtypeStruct((rows_here, HW), bf16), jax.ShapeDtypeStruct((rows_here, HW), f32)]
    att_t, lse_t, q, k, kx, vext, xl = pl.pallas_call(
        attend_first,
        grid_spec=pltpu.PrefetchScalarGridSpec(
            num_scalar_prefetch=1,
            grid=(steps,),
            in_specs=[whole((part, D))] * 4 + [whole((1, D))] + [wcol(0), wcol(1), wcol(2)]
            + [pl.BlockSpec((1, HW), lambda i, m: (0, m[0]))] * 2,
            out_specs=[thin, thin, whole(full), whole(full), whole((2, length_all, D)),
                       whole((length_all, D)), whole((length_all, D))],
        ),
        out_shape=pair + [
            jax.ShapeDtypeStruct(full, bf16),
            jax.ShapeDtypeStruct(full, bf16),
            jax.ShapeDtypeStruct((2, length_all, D), bf16),
            jax.ShapeDtypeStruct((length_all, D), bf16),
            jax.ShapeDtypeStruct((length_all, D), bf16),
        ],
        cost_estimate=cost(8 * 10 ** 9),
        name="attend_first",
    )(meta, x_own, x_far, y_own, y_far, tv, qkv_weight, qkv_weight, qkv_weight,
      row(query_bias), row(value_bias))

    theirs = lax.ppermute(att_t, "seq", beside)
    att_m, lse_m = pl.pallas_call(
        attend_second,
        grid=(steps,),
        in_specs=[thin, whole((2, length_all, D)), whole((length_all, D))],
        out_specs=[thin, thin],
        out_shape=pair,
        cost_estimate=cost(8 * 10 ** 9),
        name="attend_second",
    )(q, kx, vext)

    tiles = rows_here // RB
    half = tiles // 2
    near = pl.BlockSpec((RB, D), lambda i, m: (jnp.minimum(i, half - 1), 0))
    far = pl.BlockSpec((RB, D), lambda i, m: (jnp.maximum(i - half, 0), 0))
    tile = pl.BlockSpec((RB, D), lambda i, m: (i, 0))
    mid = pl.BlockSpec((RB, HW), lambda i, m: (i, 0))
    w_mine = pl.BlockSpec((HW, D), lambda i, m: (m[0], 0))
    w_theirs = pl.BlockSpec((HW, D), lambda i, m: (1 - m[0], 0))
    vec = whole((1, D))
    packed = (2 * ff + D) * D // HW
    output, first_grad, ag_mine, ag_theirs, big_keep, big_send, gvec = pl.pallas_call(
        middle_kernel,
        grid_spec=pltpu.PrefetchScalarGridSpec(
            num_scalar_prefetch=1,
            grid=(tiles,),
            in_specs=[near, far, near, far, vec, mid, mid, w_mine, w_theirs, vec, vec, vec,
                      whole((D, ff)), whole((1, ff)), whole((ff, D)), vec, vec, vec],
            out_specs=[tile, tile, mid, mid, whole((packed // 2, HW)), whole((packed // 2, HW)),
                       whole((16, D))],
            scratch_shapes=[pltpu.VMEM((ff, D), f32), pltpu.VMEM((D, ff), f32),
                            pltpu.VMEM((D, D), f32), pltpu.VMEM((packed, HW), bf16)],
        ),
        out_shape=[
            jax.ShapeDtypeStruct((rows_here, D), bf16),
            jax.ShapeDtypeStruct((rows_here, D), f32),
            jax.ShapeDtypeStruct((rows_here, HW), bf16),
            jax.ShapeDtypeStruct((rows_here, HW), bf16),
            jax.ShapeDtypeStruct((packed // 2, HW), bf16),
            jax.ShapeDtypeStruct((packed // 2, HW), bf16),
            jax.ShapeDtypeStruct((16, D), f32),
        ],
        cost_estimate=cost(8 * 10 ** 9),
        name="middle",
    )(meta, x_own, x_far, c_own, c_far, tv, att_m, theirs, out_weight, out_weight,
      row(out_bias), row(attn_gain), row(attn_shift), up_weight, row(up_bias), down_weight,
      row(down_bias), row(ffn_gain), row(ffn_shift))

    ag_other = lax.ppermute(ag_theirs, "seq", beside)
    big_got = lax.ppermute(big_send, "seq", beside)
    out_far = lax.ppermute(output[part:], "seq", across)

    sums = [(HW, length_all), (HW, length_all), (D, HW), (1, HW)]
    sum_shapes = [jax.ShapeDtypeStruct(a, f32) for a in sums]
    keys = [whole(full), whole((2, length_all, D)), whole((length_all, D))]
    dq_m, *partial = pl.pallas_call(
        back_first,
        grid=(steps,),
        in_specs=[thin] + keys + [pl.BlockSpec((QB, D), lambda i: (i, 0)), thin, thin],
        out_specs=[thin] + [whole(a) for a in sums],
        out_shape=[pair[0]] + sum_shapes,
        cost_estimate=cost(12 * 10 ** 9),
        name="back_first",
    )(q, k, kx, vext, xl, ag_mine, lse_m)

    big_keep, big_send = halves(add_low(big_keep, big_got), chip)
    big_got = lax.ppermute(big_send, "seq", across)

    dq_t, dk, dv, wide_keep, wide_send = pl.pallas_call(
        back_second,
        grid_spec=pltpu.PrefetchScalarGridSpec(
            num_scalar_prefetch=1,
            grid=(steps,),
            in_specs=[later] + keys + [whole((length_all, D)), thin, thin]
            + [whole(a) for a in sums] + [whole((16, D))],
            out_specs=[thin, whole(full), whole(full), whole((2 * D, HW)), whole((2 * D, HW))],
            scratch_shapes=[pltpu.VMEM(a, f32) for a in sums]
            + [pltpu.VMEM((4 * D, HW), bf16)],
        ),
        out_shape=[
            pair[0],
            jax.ShapeDtypeStruct(full, bf16),
            jax.ShapeDtypeStruct(full, bf16),
            jax.ShapeDtypeStruct((2 * D, HW), bf16),
            jax.ShapeDtypeStruct((2 * D, HW), bf16),
        ],
        cost_estimate=cost(12 * 10 ** 9),
        name="back_second",
    )(meta, q, k, kx, vext, xl, ag_other, lse_t, *partial, gvec)

    wide_got = lax.ppermute(wide_send, "seq", across)
    merged = jnp.concatenate([add_low(big_keep, big_got), add_low(wide_keep, wide_got)], 0)
    merged, dq_t, dk_t, dv_t = lax.optimization_barrier(
        (merged, dq_t, dk[rows_here:], dv[rows_here:]))
    got_q, got_k, got_v = [lax.ppermute(a, "seq", beside) for a in (dq_t, dk_t, dv_t)]
    groups = dp_groups(dp_size)
    merged = scatter_group(merged, groups[0], dp_size)
    merged, got_q, got_k, got_v = lax.optimization_barrier((merged, got_q, got_k, got_v))

    cols = [pl.BlockSpec((D, HW), lambda i, m, j=j: (0, 2 * j + m[0])) for j in range(3)]
    cols += [pl.BlockSpec((D, HW), lambda i, m, j=j: (0, 2 * j + 1 - m[0])) for j in range(3)]

    def input_part(which, kind):
        return pl.pallas_call(
            input_kernel,
            grid_spec=pltpu.PrefetchScalarGridSpec(
                num_scalar_prefetch=1,
                grid=(1,),
                in_specs=[pl.BlockSpec((part, D), lambda i, m: (which, 0))]
                + [pl.BlockSpec((part, HW), lambda i, m: (which, 0))] * 6 + cols,
                out_specs=whole((part, D)),
            ),
            out_shape=jax.ShapeDtypeStruct((part, D), kind),
            cost_estimate=cost(2 * 10 ** 9),
            name="inputs",
        )(meta, first_grad, dq_m, dk, dv, got_q, got_k, got_v, *([qkv_weight] * 6))

    def both(own, other):
        return jnp.stack([jnp.where(chip == 0, own, other), jnp.where(chip == 0, other, own)])

    grad_out = input_part(1, bf16)
    result = both(output[:part], out_far)
    for group in groups[1:]:
        merged = scatter_group(merged, group, dp_size)
    merged, grad_out = lax.optimization_barrier((merged, grad_out))
    grad_far = lax.ppermute(grad_out, "seq", across)
    grad_own = input_part(0, f32)
    for group in groups[:0:-1]:
        merged = gather_group(merged, group, dp_size)
    merged, grad_own, grad_far, result = lax.optimization_barrier(
        (merged, grad_own, grad_far, result))
    input_grad = both(grad_own, grad_far.astype(f32))
    merged = gather_group(merged, groups[0], dp_size)
    merged, input_grad = lax.optimization_barrier((merged, input_grad))
    merged_far = lax.ppermute(merged, "seq", across)
    other = lax.ppermute(merged, "seq", beside)
    other_far = lax.ppermute(merged_far, "seq", beside)
    shapes = [(ff, D), (D, ff), (D, D), (D, 3 * D), (1, ff)] + [(1, D)] * 8
    g_down, g_up, g_out, g_qkv, ubias, *vecs = pl.pallas_call(
        unpack_kernel,
        grid_spec=pltpu.PrefetchScalarGridSpec(
            num_scalar_prefetch=1,
            grid=(1,),
            in_specs=[whole(merged.shape)] * 4,
            out_specs=[whole(a) for a in shapes],
            scratch_shapes=[pltpu.VMEM((packed, HW), bf16), pltpu.VMEM((2, 4 * D, HW), bf16)],
        ),
        out_shape=[jax.ShapeDtypeStruct(a, f32) for a in shapes],
        name="unpack",
    )(meta, merged, merged_far, other, other_far)
    vecs = [a.reshape(D) for a in vecs]
    return (
        result, input_grad, g_qkv, vecs[6], vecs[7], g_out, vecs[0], vecs[1], vecs[2],
        g_up, ubias.reshape(ff), g_down, vecs[3], vecs[4], vecs[5],
    )


def solution(mesh):
    rows = P("dp", "seq", None)
    in_specs = (rows, P("dp"), P("dp")) + (P(),) * 13 + (rows,)
    out_specs = (rows, rows) + (P(),) * 13
    return jax.shard_map(body, mesh=mesh, in_specs=in_specs, out_specs=out_specs, check_vma=False)
```
